32 devices in a mesh: head: 2 (over x), expert: 16 (over z, y, core).
Axes of the slice: x: 2, y: 2, z: 4, core: 2. Of those that a mesh axis runs over, the one named last changes fastest.
Arguments:
- queries: bfloat16 [256, 128, 576], P('expert', 'head'), may hold values from -64 to 64
- resident_cache: bfloat16 [64, 256, 576], P('expert'), may hold values from -6 to 6
- resident_len: int32 [64], P('expert'), may hold values from 1 to 256, as said below
- new_cache: bfloat16 [192, 64, 576], P('expert'), may hold values from -6 to 6
- new_len: int32 [192], replicated, may hold values from 1 to 64, as said below
- new_owner: int32 [192], replicated, may hold values from 0 to 15, as said below
- value_up: bfloat16 [128, 512, 128], P('head'), may hold values from -0.25 to 0.25
- w_output: bfloat16 [16384, 7168], P('head', 'expert'), may hold values from -0.046875 to 0.046875
- residual: bfloat16 [256, 7168], P(None, 'expert'), may hold values from -6 to 6
- expert_ids: int32 [256, 8], replicated, may hold values from 0 to 15, all different within a row; in each aligned block of 16 rows (0 to 15, 16 to 31, ...) at most 12 rows name the same one
- expert_gates: float32 [256, 8], replicated, may hold values from 0.1 to 1
- norm_gain: bfloat16 [7168], replicated, may hold values from 0.5 to 1.5
- w_gate: bfloat16 [16, 7168, 1024], P('expert', None, 'head'), may hold values from -0.0625 to 0.0625
- w_up: bfloat16 [16, 7168, 1024], P('expert', None, 'head'), may hold values from -0.0625 to 0.0625
- w_down: bfloat16 [16, 1024, 7168], P('expert', 'head'), may hold values from -0.1875 to 0.1875
Outputs:
- layer_out: bfloat16 [256, 7168], P('head', 'expert')
The draws below stay inside these ranges and needn't reach their ends.
Inputs may be any that keep to these rules, and one draw needn't show every extreme that they name: `resident_len`: every decode owner has a resident request of length 256. `new_len`: every prefill device holds a new request of length 64. `new_owner`: one prefill device sends at most 2 of its 12 new requests to one decode owner, and every decode owner receives exactly 12 in all; a prefill device sends either 2 or none to each owner, except to at most one owner, which gets the remainder of 12 divided by 2. `expert_ids`: in each aligned block of 16 rows (the rows of one decode owner) no expert is named by more than 12 rows; the 8 experts of a row differ.
All inputs are finite; a program needn't handle non-finite values.
Results may differ from the reference program's by a relative error of at most 0.012.
Values may be sent and summed in bfloat16 or wider, within the bound.
A program may use at most 128 MiB of HBM per device.

```python
import math
import jax
import jax.numpy as jnp
import numpy as np
from jax import lax

D = 7168
H = 128
LAT = 512
ROPE = 64
NOPE = 128
VDIM = 128
EFF = 1024
TOPK = 8
REQ_DEV = 4
CTX = 256
NEW_DEV = 12
NEWLEN = 64
EXPERTS = 16
ROWS_DEV = 16
ROWS = 256
REQS = 64
NEWS = 192
MOST = 2
CAP = 12
N_EXPERT = 16


def draw_queries(key, part):
    values = jax.random.normal(key, (ROWS, H, LAT + ROPE), jnp.float32)
    return jnp.clip(values, -64.0, 64.0).astype(jnp.bfloat16)


def draw_resident_len(key, part):
    base = jax.random.randint(key, (N_EXPERT, REQ_DEV), 1, CTX + 1)
    chosen = jax.random.randint(jax.random.fold_in(key, 3), (N_EXPERT, 1), 0, REQ_DEV)
    longest = jnp.arange(REQ_DEV)[None, :] == chosen
    return jnp.where(longest, CTX, base).reshape(REQS).astype(jnp.int32)


def draw_new_len(key, part):
    base = jax.random.randint(key, (N_EXPERT, NEW_DEV), 1, NEWLEN + 1)
    chosen = jax.random.randint(jax.random.fold_in(key, 5), (N_EXPERT, 1), 0, NEW_DEV)
    longest = jnp.arange(NEW_DEV)[None, :] == chosen
    return jnp.where(longest, NEWLEN, base).reshape(NEWS).astype(jnp.int32)


def draw_new_owner(key, part):
    spread = jax.random.permutation(jax.random.fold_in(key, 11), N_EXPERT)
    shifted = jax.random.permutation(jax.random.fold_in(key, 12), N_EXPERT)
    offsets = jax.random.permutation(jax.random.fold_in(key, 13), N_EXPERT)
    labels = jax.vmap(lambda one: jax.random.permutation(one, NEW_DEV))(jax.random.split(jax.random.fold_in(key, 14), N_EXPERT))
    groups = labels // MOST
    target = (shifted[:, None] + offsets[groups]) % N_EXPERT
    return spread[target].reshape(NEWS).astype(jnp.int32)


def level_of(own_key, shape, pieces, least, top_value):
    def one(position, shards_of):
        steps = jax.random.uniform(jax.random.fold_in(jax.random.fold_in(own_key, 6), position), (shards_of,), jnp.float32, least / len(pieces), top_value / len(pieces))
        return jnp.repeat(jnp.exp(steps), shape[position] // shards_of).reshape((-1,) + (1,) * (len(shape) - position - 1))

    level = one(*pieces[0])
    for cut in pieces[1:]:
        level = level * one(*cut)
    return level


def shared_out(own_key, own, number, rows, amount, top, limit, slope):
    order = jax.random.permutation(own_key, amount)
    crowded, usual = shares(amount, rows * top, limit, slope, True), shares(amount, rows * top, limit, slope, False)
    places = jnp.arange(amount)

    def named(lengths, offset_by):
        used = int((lengths > 0).sum())
        fixed = max(1, used // 4)
        moved = fixed + (places - fixed + offset_by * (used - fixed)) % max(1, amount - fixed)
        return jnp.zeros((amount,), jnp.int32).at[order[jnp.where(places < fixed, places, moved)]].set(jnp.asarray(lengths, jnp.int32))

    lengths = jnp.where(number % 4 == 0, named(crowded, number // 4), named(usual, number - number // 4 - 1))
    mixed = jax.random.permutation(jax.random.fold_in(own, 3), amount)
    source_of, receiver = mixed[0:amount // 2 * 2:2], mixed[1:amount // 2 * 2:2]
    margin = jnp.minimum(lengths[source_of] - 1, limit - lengths[receiver]) // 2
    margin = jnp.where((source_of == order[0]) | (receiver == order[0]) | (lengths[receiver] == 0), 0, jnp.maximum(margin, 0))
    moved = jax.random.randint(jax.random.fold_in(own, 4), (amount // 2,), 0, 1 << 20) % (margin + 1)
    lengths = lengths.at[source_of].add(-moved).at[receiver].add(moved)
    members = jnp.searchsorted(jnp.cumsum(lengths), jnp.arange(rows * top), side="right").astype(jnp.int32)
    grid = members.reshape(top, rows).T
    grid = grid[jax.random.permutation(jax.random.fold_in(own, 1), rows)]
    offset_by = jax.random.randint(jax.random.fold_in(own, 2), (rows, 1), 0, top)
    return jnp.take_along_axis(grid, (jnp.arange(top)[None, :] + offset_by) % top, axis=1)


def shares(amount, total, reach, slope, full):
    portions = [(1 << 20) // math.isqrt(grade ** slope) + 1 for grade in range(1, amount + 1)]
    largest = reach if full else min(reach, max(-(-total // amount), total * portions[0] // sum(portions)))
    least = 1 if total - largest >= amount - 1 else 0
    holding, rest = [largest] + [least] * (amount - 1), total - largest - least * (amount - 1)
    while rest > 0:
        candidates = [i for i in range(1, amount) if holding[i] < largest] or [i for i in range(1, amount) if holding[i] < reach]
        whole, left = sum([portions[i] for i in candidates]), rest
        for i in candidates:
            addition = min(reach - holding[i], max(1, left * portions[i] // whole), rest)
            holding[i] = holding[i] + addition
            rest = rest - addition
    return np.array(holding)


def noise(key, dims, width, limit, shards=(), kind=jnp.bfloat16):
    entries = width * jax.random.normal(key, dims, jnp.float32)
    if shards:
        entries = entries * level_of(key, dims, shards, -0.22, 0.18)
    return jnp.clip(entries, -limit, limit).astype(kind)


def setup_inputs(seed: int = 0) -> dict:
    key_list = jax.random.split(jax.random.key(seed), 16)
    queries = draw_queries(jax.random.fold_in(key_list[15], 71), 0)
    resident_cache = noise(key_list[1], (REQS, CTX, LAT + ROPE), 1.0, 6.0, ((0, 16),))
    resident_len = draw_resident_len(jax.random.fold_in(key_list[15], 71), 0)
    new_cache = noise(key_list[3], (NEWS, NEWLEN, LAT + ROPE), 1.0, 6.0, ((0, 16),))
    new_len = draw_new_len(jax.random.fold_in(key_list[15], 71), 0)
    new_owner = draw_new_owner(jax.random.fold_in(key_list[15], 71), 0)
    value_up = noise(key_list[6], (H, LAT, VDIM), LAT ** -0.5, 0.25, ((0, 2),))
    w_output = noise(key_list[7], (H * VDIM, D), (H * VDIM) ** -0.5, 0.046875, ((0, 2), (1, 16)))
    residual = noise(key_list[8], (ROWS, D), 1.0, 6.0, ((1, 16),))
    expert_ids_keys = jax.random.split(jax.random.fold_in(key_list[9], 1), ROWS // ROWS_DEV)
    expert_ids_turns = jax.random.permutation(jax.random.fold_in(key_list[9], 3), ROWS // ROWS_DEV)
    expert_ids = jax.vmap(lambda own, number: shared_out(jax.random.fold_in(key_list[9], 2), own, number, ROWS_DEV, EXPERTS, TOPK, CAP, 2))(expert_ids_keys, expert_ids_turns).reshape((ROWS, TOPK))
    expert_gates = jnp.clip(jnp.exp(jax.random.uniform(key_list[10], (ROWS, TOPK), jnp.float32, math.log(0.1), math.log(1.0))), 0.1, 1.0)
    norm_gain = jnp.clip(1.0 + 0.1 * jax.random.normal(key_list[11], (D,), jnp.float32), 0.5, 1.5).astype(jnp.bfloat16)
    w_gate = noise(key_list[12], (EXPERTS, D, EFF), D ** -0.5, 0.0625, ((0, 16), (2, 2)))
    w_up = noise(key_list[13], (EXPERTS, D, EFF), D ** -0.5, 0.0625, ((0, 16), (2, 2)))
    w_down = noise(key_list[14], (EXPERTS, EFF, D), EFF ** -0.5, 0.1875, ((0, 16), (1, 2)))
    return {"queries": queries, "resident_cache": resident_cache, "resident_len": resident_len, "new_cache": new_cache, "new_len": new_len, "new_owner": new_owner, "value_up": value_up, "w_output": w_output, "residual": residual, "expert_ids": expert_ids, "expert_gates": expert_gates, "norm_gain": norm_gain, "w_gate": w_gate, "w_up": w_up, "w_down": w_down}


def attend(queries, caches, length, value_up):
    inverse_root = (NOPE + ROPE) ** (-0.5)
    scores = jnp.einsum('rhc,rtc->rht', queries.astype(jnp.float32), caches.astype(jnp.float32)) * inverse_root
    inside = jnp.arange(caches.shape[1], dtype=jnp.int32)[None, None, :] < length[:, None, None]
    scores = jnp.where(inside, scores, -jnp.inf)
    highest = lax.optimization_barrier(jnp.max(scores, axis=2, keepdims=True))
    raised = jnp.exp(scores - highest)
    weights = (raised / lax.optimization_barrier(jnp.sum(raised, axis=2, keepdims=True))).astype(jnp.bfloat16)
    latent = jnp.einsum('rht,rtc->rhc', weights.astype(jnp.float32), caches[:, :, :LAT].astype(jnp.float32)).astype(jnp.bfloat16)
    values = jnp.einsum('rhc,hcv->rhv', latent.astype(jnp.float32), value_up.astype(jnp.float32)).astype(jnp.bfloat16)
    return values.reshape(values.shape[0], H * VDIM)

def reference(queries, resident_cache, resident_len, new_cache, new_len, new_owner, value_up, w_output, residual, expert_ids, expert_gates, norm_gain, w_gate, w_up, w_down):
    blocks = queries.reshape(N_EXPERT, ROWS_DEV, H, LAT + ROPE)
    ordering = jnp.argsort(new_owner, stable=True).astype(jnp.int32)
    resident_att = attend(blocks[:, :REQ_DEV].reshape(REQS, H, LAT + ROPE), resident_cache, resident_len, value_up)
    arrived_att = attend(blocks[:, REQ_DEV:].reshape(NEWS, H, LAT + ROPE), new_cache[ordering], new_len[ordering], value_up)
    attention = jnp.concatenate([resident_att.reshape(N_EXPERT, REQ_DEV, H * VDIM), arrived_att.reshape(N_EXPERT, NEW_DEV, H * VDIM)], axis=1).reshape(ROWS, H * VDIM)
    mixed = jnp.dot(attention, w_output, preferred_element_type=jnp.float32)
    hidden = (residual.astype(jnp.float32) + mixed).astype(jnp.bfloat16)
    picks = expert_ids.reshape(N_EXPERT, ROWS_DEV * TOPK)
    onehot = (picks[:, :, None] == jnp.arange(EXPERTS, dtype=jnp.int32)[None, None, :]).astype(jnp.int32)
    ranking = (lax.optimization_barrier(jnp.sum(jnp.cumsum(onehot, axis=1) * onehot, axis=2)) - 1).astype(jnp.int32)
    source = jnp.arange(N_EXPERT, dtype=jnp.int32)[:, None]
    slot_index = (picks * (N_EXPERT * CAP) + source * CAP + ranking).astype(jnp.int32)
    row_index = (source * ROWS_DEV + jnp.arange(ROWS_DEV * TOPK, dtype=jnp.int32)[None, :] // TOPK).astype(jnp.int32)
    slot_rows = jnp.full((EXPERTS * N_EXPERT * CAP,), ROWS, jnp.int32).at[slot_index.reshape(-1)].set(row_index.reshape(-1))
    padded = jnp.concatenate([hidden, jnp.zeros((1, D), jnp.bfloat16)], axis=0)
    inputs_all = padded[slot_rows].reshape(EXPERTS, N_EXPERT * CAP, D)

    def apply_expert(operands):
        inputs, gate_weight, up_weight, down_weight = operands
        values = inputs.astype(jnp.float32)
        inverse = lax.rsqrt(lax.optimization_barrier(jnp.mean(values * values, axis=1, keepdims=True)) + 1e-06)
        normed = (values * inverse * norm_gain.astype(jnp.float32)).astype(jnp.bfloat16)
        gate_act = jnp.dot(normed, gate_weight, preferred_element_type=jnp.float32)
        up_act = jnp.dot(normed, up_weight, preferred_element_type=jnp.float32)
        hidden_act = (jax.nn.silu(gate_act) * up_act).astype(jnp.bfloat16)
        return jnp.dot(hidden_act, down_weight, preferred_element_type=jnp.float32)
    expert_out = lax.map(apply_expert, (inputs_all, w_gate, w_up, w_down))
    picked = expert_out.reshape(EXPERTS * N_EXPERT * CAP, D)[slot_index.reshape(ROWS, TOPK)]
    routed = lax.optimization_barrier(jnp.sum(picked * expert_gates[:, :, None], axis=1))
    return (hidden.astype(jnp.float32) + routed).astype(jnp.bfloat16)
```

```python
import jax
import jax.numpy as jnp
from jax import lax
from jax.sharding import PartitionSpec as P

ROPE = 64
NOPE = 128


def attend(queries, caches, length, value_up):
    inverse_root = (NOPE + ROPE) ** (-0.5)
    latent_width = value_up.shape[1]
    scores = (
        jnp.einsum("rhc,rtc->rht", queries, caches, preferred_element_type=jnp.float32)
        * inverse_root
    )
    inside = lax.broadcasted_iota(jnp.int32, scores.shape, 2) < length[:, None, None]
    scores = jnp.where(inside, scores, -jnp.inf)
    highest = jnp.max(scores, axis=2, keepdims=True)
    raised = jnp.exp(scores - highest)
    weights = (raised / jnp.sum(raised, axis=2, keepdims=True)).astype(jnp.bfloat16)
    latent = jnp.einsum(
        "rht,rtc->rhc", weights, caches[:, :, :latent_width], preferred_element_type=jnp.float32
    ).astype(jnp.bfloat16)
    values = jnp.einsum(
        "rhc,hcv->rhv", latent, value_up, preferred_element_type=jnp.float32
    ).astype(jnp.bfloat16)
    return values.reshape(values.shape[0], -1)


def earlier_equal(labels):
    count = labels.shape[0]
    position = jnp.arange(count, dtype=jnp.int32)
    before = (labels[:, None] == labels[None, :]) & (position[None, :] < position[:, None])
    return jnp.sum(before.astype(jnp.int32), axis=1)


def per_device(
    queries,
    resident_cache,
    resident_len,
    new_cache,
    new_len,
    new_owner,
    value_up,
    w_output,
    residual,
    expert_ids,
    expert_gates,
    norm_gain,
    w_gate,
    w_up,
    w_down,
):
    n_expert = lax.axis_size("expert")
    n_head = lax.axis_size("head")
    owner_index = lax.axis_index("expert")
    head_index = lax.axis_index("head")
    req_count = resident_cache.shape[0]
    new_count, new_span, cache_width = new_cache.shape
    rows_dev = req_count + new_count
    rows_all = rows_dev * n_expert
    local_experts = w_gate.shape[0]
    most = max(2, (4 * new_count + 3 * n_expert - 1) // (3 * n_expert))
    block_rows = rows_all // n_head
    piece = new_span // n_head

    targets = lax.dynamic_slice_in_dim(new_owner, owner_index * new_count, new_count)
    places = targets * most + earlier_equal(targets)
    slots = jnp.arange(n_expert * most, dtype=jnp.int32)
    senders = jnp.sum(
        jnp.where(
            places[None, :] == slots[:, None], jnp.arange(new_count, dtype=jnp.int32)[None, :], 0
        ),
        axis=1,
    )
    share = lax.dynamic_slice_in_dim(new_cache, head_index * piece, piece, axis=1)
    outgoing = jnp.take(share, senders, axis=0, mode="clip").reshape(
        n_expert, most, piece, cache_width
    )
    incoming = lax.all_to_all(outgoing, "expert", split_axis=0, concat_axis=0, tiled=True)
    position = jnp.arange(new_owner.shape[0], dtype=jnp.int32)
    named = new_owner == owner_index
    before = jnp.sum((named[None, :] & (position[None, :] < position[:, None])).astype(jnp.int32), 1)
    chosen = jnp.sum(
        jnp.where(
            named[None, :]
            & (before[None, :] == jnp.arange(new_count, dtype=jnp.int32)[:, None]),
            position[None, :],
            0,
        ),
        axis=1,
    )
    anchor = chosen // new_count
    arrived_share = jnp.take(
        incoming.reshape(n_expert * most, piece, cache_width),
        anchor * most + earlier_equal(anchor),
        axis=0,
        mode="clip",
    )
    arrived = lax.all_gather(arrived_share, "head", axis=1, tiled=True)
    resident_att = attend(queries[:req_count], resident_cache, resident_len, value_up)
    arrived_att = attend(queries[req_count:], arrived, new_len[chosen], value_up)
    attention = jnp.concatenate([resident_att, arrived_att], axis=0)
    mixed = jnp.dot(
        lax.all_gather(attention, "expert", axis=0, tiled=True),
        w_output,
        preferred_element_type=jnp.float32,
    ).T
    swap = [(0, 1), (1, 0)]
    if n_head == 2:
        mixed = mixed.astype(jnp.bfloat16)
        summed = mixed.astype(jnp.float32) + lax.ppermute(mixed, "head", swap).astype(jnp.float32)
    else:
        summed = lax.psum(mixed, "head")
    hidden = (residual.T.astype(jnp.float32) + summed).astype(jnp.bfloat16)
    hidden_block = lax.dynamic_slice_in_dim(hidden, head_index * block_rows, block_rows, axis=1)

    inputs = lax.all_gather(hidden, "expert", axis=0, tiled=True).astype(jnp.float32)
    inverse = lax.rsqrt(jnp.mean(inputs * inputs, axis=0, keepdims=True) + 1e-06)
    normed = (inputs * inverse * norm_gain.astype(jnp.float32)[:, None]).astype(jnp.bfloat16)
    partial = None
    for e in range(local_experts):
        gate_act = jnp.einsum("df,dr->fr", w_gate[e], normed, preferred_element_type=jnp.float32)
        up_act = jnp.einsum("df,dr->fr", w_up[e], normed, preferred_element_type=jnp.float32)
        act = (jax.nn.silu(gate_act) * up_act).astype(jnp.bfloat16)
        down = jnp.einsum("fd,fr->dr", w_down[e], act, preferred_element_type=jnp.float32)
        mine = expert_ids == owner_index * local_experts + e
        weight = jnp.sum(jnp.where(mine, expert_gates, 0.0), axis=1)
        term = down * weight[None, :]
        partial = term if partial is None else partial + term
    routed = lax.psum_scatter(
        partial.astype(jnp.bfloat16), "expert", scatter_dimension=0, tiled=True
    )
    if n_head == 2:
        kept = lax.dynamic_slice_in_dim(routed, head_index * block_rows, block_rows, axis=1)
        sent = lax.dynamic_slice_in_dim(routed, (1 - head_index) * block_rows, block_rows, axis=1)
        got = lax.ppermute(sent, "head", swap)
        routed_block = kept.astype(jnp.float32) + got.astype(jnp.float32)
    else:
        routed_block = lax.psum_scatter(
            routed, "head", scatter_dimension=1, tiled=True
        ).astype(jnp.float32)
    return (hidden_block.astype(jnp.float32) + routed_block).astype(jnp.bfloat16).T


def solution(mesh):
    return jax.shard_map(
        per_device,
        mesh=mesh,
        in_specs=(
            P("expert", "head", None),
            P("expert", None, None),
            P("expert"),
            P("expert", None, None),
            P(),
            P(),
            P("head", None, None),
            P("head", "expert"),
            P(None, "expert"),
            P(),
            P(),
            P(),
            P("expert", None, "head"),
            P("expert", None, "head"),
            P("expert", "head", None),
        ),
        out_specs=P("head", "expert"),
        check_vma=False,
    )
```
